256 devices in a mesh: row: 16 (over y_lo, x, core), col: 16 (over z, y_hi).
Axes of the slice: x: 4, y: 4 (y_hi: 2, y_lo: 2; y = y_hi * 2 + y_lo), z: 8, core: 2. Of those that a mesh axis runs over, the one named last changes fastest.
Arguments:
- vector: float32 [8192, 8192], P('row', 'col'), may hold values from -6 to 6
- one_electron: float32 [16, 16], replicated, may hold values from -0.18 to 0.18
- links: int32 [64, 8], replicated, may hold values from 0 to 63, as said below
- counts: int32 [64], replicated, may hold values from 4 to 8, as said below
- pairs: int32 [64, 8], P('row'), may hold values from 0 to 255
- signs: int32 [64, 8, 128, 128], P('row'), may hold values from -1 to 1
Outputs:
- sigma_vector: float32 [8192, 8192], P('row', 'col')
The draws below stay inside these ranges and needn't reach their ends.
Inputs may be any that keep to these rules, and one draw needn't show every extreme that they name: `links`: entries name string blocks; only the first counts[I] entries of block I are used. Counting used entries only, the blocks I with I // 4 = d name blocks K with K // 4 = s at most 2 times for any d and s, and some pair d, s reaches 2. Block I has counts[I] used links; every block I with I % 4 = 0 has 8.
All inputs are finite; a program needn't handle non-finite values.
Results may differ from the reference program's by a relative error of at most 0.000051.
Values sent between devices are 32-bit elements; how exact they have to be, the bound alone decides.
No kernel may reach another device: no remote copies, remote signals or barrier semaphores. Data moves between devices by JAX's collectives and lax.ppermute only.
A program may use at most 128 MiB of HBM per device.

```python
import jax
import jax.numpy as jnp
from jax import lax

BLK = 128
NORB = 16
LMAX = 8
A_DEV = 4
NPAIR = 256
NBLK_A = 64
NA = 8192


def link_tables(key, salt, blocks_all, blocks_dev, link_max):
    key = jax.random.fold_in(key, salt)
    count_key, order_key, local_key = jax.random.split(key, 3)
    devices = blocks_all // blocks_dev
    slot_width = blocks_dev * link_max
    capacity = (slot_width + devices - 1) // devices
    used = jax.random.randint(count_key, (blocks_all,), link_max // 2, link_max + 1)
    first_block = jnp.arange(blocks_all, dtype=jnp.int32) % blocks_dev == 0
    used = jnp.where(first_block, link_max, used).astype(jnp.int32)
    in_use = (jnp.arange(link_max, dtype=jnp.int32)[None, :] < used[:, None]).reshape(devices, slot_width)
    position = jnp.cumsum(in_use.astype(jnp.int32), axis=1) - 1
    position = jnp.clip(position, 0, slot_width - 1)

    def one_order(order_seed):
        return jax.random.permutation(order_seed, devices)
    orders = jax.vmap(one_order)(jax.random.split(order_key, devices)).astype(jnp.int32)
    sources = jnp.take_along_axis(orders, position // capacity, axis=1)
    local_block = jax.random.randint(local_key, (devices, slot_width), 0, blocks_dev)
    link_table = (sources * blocks_dev + local_block).reshape(blocks_all, link_max)
    return (link_table.astype(jnp.int32), used)


def draw_links(key, part):
    return link_tables(key, 11, NBLK_A, A_DEV, LMAX)[0]


def draw_counts(key, part):
    return link_tables(key, 11, NBLK_A, A_DEV, LMAX)[1]


def with_ends(result, key, low, largest):
    longest = result.shape.index(max(result.shape))
    spots = []
    for shift in (0, 1):
        where = [jax.random.randint(jax.random.fold_in(key, axis), (), 0, length) for axis, length in enumerate(result.shape)]
        where[longest] = (where[longest] + shift) % result.shape[longest]
        spots.append(tuple(where))
    return result.at[spots[0]].set(low).at[spots[1]].set(largest)


def steps_of(stream_key, dims, shards, least, largest):
    level, own = 1.0, jax.random.fold_in(stream_key, 6)
    for dim, blocks in shards:
        steps = jnp.exp(jax.random.uniform(jax.random.fold_in(own, dim), (blocks,), jnp.float32, least / len(shards), largest / len(shards)))
        level = level * jnp.repeat(steps, dims[dim] // blocks).reshape([-1 if axis == dim else 1 for axis in range(len(dims))])
    return level


def noise(stream_key, shape, scale, reach, shards=(), held_as=jnp.bfloat16):
    result = scale * jax.random.normal(stream_key, shape, jnp.float32)
    if shards:
        result = result * steps_of(stream_key, shape, shards, -0.22, 0.18)
    return jnp.clip(result, -reach, reach).astype(held_as)


def setup_inputs(seed: int = 0) -> dict:
    seeds = jax.random.split(jax.random.key(seed), 7)
    return {
        "vector": noise(seeds[0], (NA, NA), 1.0, 6.0, ((0, 16), (1, 16)), jnp.float32),
        "one_electron": noise(seeds[1], (NORB, NORB), 0.03, 0.18, (), jnp.float32),
        "links": draw_links(jax.random.fold_in(seeds[6], 71), 0),
        "counts": draw_counts(jax.random.fold_in(seeds[6], 71), 0),
        "pairs": with_ends(jax.random.randint(seeds[4], (NBLK_A, LMAX), 0, NPAIR), jax.random.fold_in(seeds[4], 1), 0, NPAIR - 1).astype(jnp.int32),
        "signs": with_ends(jax.random.randint(seeds[5], (NBLK_A, LMAX, BLK, BLK), -1, 2), jax.random.fold_in(seeds[5], 1), -1, 1).astype(jnp.int32),
    }


def pair_values(pair_ids, used, integrals):
    flat_table = integrals.reshape(-1)
    values = flat_table[pair_ids]
    in_use = jnp.arange(pair_ids.shape[1], dtype=jnp.int32)[None, :] < used[:, None]
    return jnp.where(in_use, values, jnp.zeros_like(values))


def reference(vector, one_electron, links, counts, pairs, signs):
    replace = pair_values(pairs, counts, one_electron)[:, :, None, None] * signs.astype(jnp.float32)
    row_tiles = vector.reshape(NBLK_A, BLK, NA)
    column_blocks = vector.reshape(NA, NBLK_A, BLK)

    def alpha_block(inputs):
        link_row, replace_row = inputs
        fetched = row_tiles[link_row]
        return jnp.einsum("lmk,lkb->mb", replace_row, fetched, precision=lax.Precision.HIGHEST)

    def beta_block(inputs):
        link_row, replace_row = inputs
        fetched = column_blocks[:, link_row, :]
        return jnp.einsum("alk,lmk->am", fetched, replace_row, precision=lax.Precision.HIGHEST)

    sigma_alpha = lax.map(alpha_block, (links, replace)).reshape(NA, NA)
    sigma_beta = lax.map(beta_block, (links, replace))
    sigma_beta = jnp.transpose(sigma_beta, (1, 0, 2)).reshape(NA, NA)
    return sigma_alpha + sigma_beta
```

```python
import functools

import jax
import jax.numpy as jnp
from jax import lax
from jax.experimental import pallas as pl
from jax.experimental.pallas import tpu as pltpu
from jax.sharding import Mesh, PartitionSpec as P

AXES = ("yl", "x", "c", "z", "yh")
SIZES = (2, 4, 2, 8, 2)
ROW = ("yl", "x", "c")
COL = ("z", "yh")
B = 128
VMEM_LIMIT = 56 * 1024 * 1024


def flat(yl, x, c, z, yh):
    return (((yl * 4 + x) * 2 + c) * 8 + z) * 2 + yh


def shift(value, axis, by):
    n = SIZES[AXES.index(axis)]
    return lax.ppermute(value, axis, [(i, (i + by) % n) for i in range(n)])


def scatter_pairs(dy, dx):
    pairs = []
    for z in range(8):
        ys, xs = z >> 2, z & 3
        for yh in range(2):
            for c in range(2):
                pairs.append((flat(ys, xs, c, z, yh), flat(ys ^ dy, (xs + dx) % 4, c, z, yh)))
    return pairs


def pair_values(pair_ids, used, integrals):
    flat_table = integrals.reshape(-1)
    onehot = pair_ids[:, :, None] == jnp.arange(flat_table.shape[0], dtype=jnp.int32)[None, None, :]
    values = jnp.sum(jnp.where(onehot, flat_table[None, None, :], 0.0), axis=2)
    in_use = jnp.arange(pair_ids.shape[1], dtype=jnp.int32)[None, :] < used[:, None]
    return jnp.where(in_use, values, 0.0)


def halves(value):
    high = value.astype(jnp.bfloat16)
    low = (value - high.astype(jnp.float32)).astype(jnp.bfloat16)
    return high, low


def phase_and_size(table):
    size = jnp.max(jnp.max(jnp.abs(table), axis=0, keepdims=True), axis=1, keepdims=True)
    phase = jnp.where(table > 0, 1.0, jnp.where(table < 0, -1.0, 0.0)).astype(jnp.bfloat16)
    return phase, size


def beta_kernel(place, links, columns, tables, out, left, right):
    step = pl.program_id(0)
    yh, which = place[1], place[2]
    block = (place[0] * 2 + which) * 4 + step
    rows = out.shape[0]
    for l in range(8):
        source = links[block, l]
        owner = source >> 2
        slot = step * 8 + l
        part = slot >> 2
        at = (((part >> 2) ^ place[3]) * 8 + (((part & 3) + place[4]) & 3) * 2 + which) * 4 + (slot & 3)
        phase, size = phase_and_size(tables[at])
        size = size * jnp.where((owner & 1) == yh, 1.0, 0.0)
        lanes = pl.ds(pl.multiple_of((source & 3) * B, B), B)
        high, low = halves(columns[owner >> 1, :, lanes] * size)
        left[:, 2 * l * B:(2 * l + 1) * B] = high
        left[:, (2 * l + 1) * B:(2 * l + 2) * B] = low
        right[:, 2 * l * B:(2 * l + 1) * B] = phase
        right[:, (2 * l + 1) * B:(2 * l + 2) * B] = phase
    out[...] = lax.dot_general(left[...], right[...], (((1,), (1,)), ((), ())), preferred_element_type=jnp.float32)


def beta_part(place, links, columns, tables):
    rows = columns.shape[1]
    return pl.pallas_call(
        beta_kernel,
        out_shape=jax.ShapeDtypeStruct((rows, 4 * B), jnp.float32),
        grid_spec=pltpu.PrefetchScalarGridSpec(
            num_scalar_prefetch=2,
            grid=(4,),
            in_specs=[
                pl.BlockSpec(columns.shape, lambda i, *_: (0, 0, 0), pipeline_mode=pl.Buffered(1)),
                pl.BlockSpec(tables.shape, lambda i, *_: (0, 0, 0), pipeline_mode=pl.Buffered(1)),
            ],
            out_specs=pl.BlockSpec((rows, B), lambda i, *_: (0, i)),
            scratch_shapes=[pltpu.VMEM((rows, 16 * B), jnp.bfloat16), pltpu.VMEM((B, 16 * B), jnp.bfloat16)],
        ),
        compiler_params=pltpu.CompilerParams(dimension_semantics=("arbitrary",), vmem_limit_bytes=VMEM_LIMIT),
        cost_estimate=pl.CostEstimate(flops=4 * rows * B * 16 * B * 2, bytes_accessed=columns.size * 4 + tables.size * 4, transcendentals=0),
        name="beta",
    )(place, links, columns, tables)


def alpha_kernel(place, links, mine, other, *rest):
    pieces, (out_other, out_mine, held, left, right, sems) = rest[:10], rest[10:]
    step = pl.program_id(0)
    spots = [(0, 0, 512), (3, 0, 512), (1, 0, 512), (2, 0, 256), (2, 256, 256), (4, 0, 512), (7, 0, 512), (5, 0, 512), (6, 0, 256), (6, 256, 256)]
    copies = [
        pltpu.make_async_copy(piece, held.at[slot, pl.ds(start, size), :], sems.at[i])
        for i, (piece, (slot, start, size)) in enumerate(zip(pieces, spots))
    ]

    @pl.when(step == 0)
    def _():
        for copy in copies:
            copy.start()
        for copy in copies:
            copy.wait()

    yl, x, c = place[0], place[1], place[2]

    def product(table, core, number, out):
        block = (yl * 8 + x * 2 + core) * 4 + number
        for l in range(8):
            source = links[block, l]
            chip = source >> 3
            slot = ((chip >> 2) ^ yl) * 4 + (((chip & 3) - x) & 3)
            phase, size = phase_and_size(table[number * 8 + l])
            size = size * jnp.where(((source >> 2) & 1) == c, 1.0, 0.0)
            rows = pl.ds(pl.multiple_of((source & 3) * B, B), B)
            high, low = halves(held[slot, rows, :] * size)
            right[2 * l * B:(2 * l + 1) * B, :] = high
            right[(2 * l + 1) * B:(2 * l + 2) * B, :] = low
            left[:, 2 * l * B:(2 * l + 1) * B] = phase
            left[:, (2 * l + 1) * B:(2 * l + 2) * B] = phase
        out[pl.ds(pl.multiple_of(number * B, B), B), :] = jnp.dot(left[...], right[...], preferred_element_type=jnp.float32)

    @pl.when(step < 4)
    def _():
        product(other, 1 - c, step, out_other)

    @pl.when(step >= 4)
    def _():
        product(mine, c, step - 4, out_mine)


def alpha_part(place, links, mine, other, pieces):
    whole = pl.BlockSpec((32, B, B), lambda i, *_: (0, 0, 0), pipeline_mode=pl.Buffered(1))
    result = pl.BlockSpec((4 * B, 4 * B), lambda i, *_: (0, 0))
    return pl.pallas_call(
        alpha_kernel,
        out_shape=[jax.ShapeDtypeStruct((4 * B, 4 * B), jnp.float32)] * 2,
        grid_spec=pltpu.PrefetchScalarGridSpec(
            num_scalar_prefetch=2,
            grid=(8,),
            in_specs=[whole, whole] + [pl.BlockSpec(memory_space=pl.ANY)] * 10,
            out_specs=[result, result],
            scratch_shapes=[
                pltpu.VMEM((8, 4 * B, 4 * B), jnp.float32),
                pltpu.VMEM((B, 16 * B), jnp.bfloat16),
                pltpu.VMEM((16 * B, 4 * B), jnp.bfloat16),
                pltpu.SemaphoreType.DMA((10,)),
            ],
        ),
        compiler_params=pltpu.CompilerParams(dimension_semantics=("arbitrary",), vmem_limit_bytes=VMEM_LIMIT),
        cost_estimate=pl.CostEstimate(flops=8 * 4 * B * B * 16 * B * 2, bytes_accessed=14 << 20, transcendentals=0),
        name="alpha",
    )(place, links, mine, other, *pieces)


CHUNKS = ((0, 256), (256, 256))


def local(vector, one_electron, links, counts, pairs, signs):
    yl, x, c, z, yh = (lax.axis_index(a) for a in AXES)
    row_index = (yl * 4 + x) * 2 + c

    from_left = shift(vector, "x", 1)
    from_right = shift(vector, "x", -1)
    from_y = shift(vector, "yl", 1)

    local_counts = lax.dynamic_slice_in_dim(counts, row_index * 4, 4)
    replace = (pair_values(pairs, local_counts, one_electron)[:, :, None, None] * signs.astype(jnp.float32)).reshape(32, B, B)
    replace_other = shift(replace, "c", 1)

    ys, xs = z >> 2, z & 3
    is_source = (yl == ys) & (x == xs)
    part = jnp.where(is_source, replace[:4], 0.0)
    for j in range(1, 8):
        part = part + lax.ppermute(replace[4 * j:4 * j + 4], AXES, scatter_pairs(j >> 2, j & 3))

    gathered = []
    tables = None
    for n, (start, size) in enumerate(CHUNKS):
        gathered.append(lax.all_gather(vector[start:start + size], "z", axis=0))
        if n == 0:
            tables = lax.all_gather(part, ROW, axis=0, tiled=True)

    across_top = shift(from_left[:256], "x", 1)
    across_low = shift(from_right[256:], "x", -1)
    y_left = shift(from_y, "x", 1)
    y_right = shift(from_y, "x", -1)
    y_across_top = shift(across_top, "yl", 1)
    y_across_low = shift(across_low, "yl", 1)

    alpha_place = jnp.stack([yl, x, c]).astype(jnp.int32)
    pieces = (vector, from_left, from_right, across_top, across_low, from_y, y_left, y_right, y_across_top, y_across_low)
    alpha_other, alpha_mine = alpha_part(alpha_place, links, replace, replace_other, pieces)
    alpha = alpha_mine + shift(alpha_other, "c", 1)

    theirs, ours = [], []
    for columns in gathered:
        place = jnp.stack([z, yh, 1 - yh, ys, xs]).astype(jnp.int32)
        theirs.append(shift(beta_part(place, links, columns, tables), "yh", 1))
        place = jnp.stack([z, yh, yh, ys, xs]).astype(jnp.int32)
        ours.append(beta_part(place, links, columns, tables))
    return jnp.concatenate([alpha[s:s + n] + o + t for (s, n), o, t in zip(CHUNKS, ours, theirs)], axis=0)


def solution(mesh):
    fine = Mesh(mesh.devices.reshape(SIZES), AXES)
    in_specs = (P(ROW, COL), P(), P(), P(), P(ROW, None), P(ROW, None, None, None))
    return jax.shard_map(local, mesh=fine, in_specs=in_specs, out_specs=P(ROW, COL), check_vma=False)
```

```python
import functools

import jax
import jax.numpy as jnp
from jax import lax
from jax.experimental import pallas as pl
from jax.experimental.pallas import tpu as pltpu
from jax.sharding import Mesh, PartitionSpec as P

AXES = ("yl", "x", "c", "z", "yh")
SIZES = (2, 4, 2, 8, 2)
ROW = ("yl", "x", "c")
COL = ("z", "yh")
B = 128
VMEM_LIMIT = 56 * 1024 * 1024


def flat(yl, x, c, z, yh):
    return (((yl * 4 + x) * 2 + c) * 8 + z) * 2 + yh


def spread(value, moves):
    pairs = []
    for z in range(8):
        ys, xs = z >> 2, z & 3
        for yh in range(2):
            for c in range(2):
                for (ay, ax), (by, bx) in moves:
                    pairs.append((flat(ys ^ ay, (xs + ax) % 4, c, z, yh), flat(ys ^ by, (xs + bx) % 4, c, z, yh)))
    return lax.ppermute(value, AXES, pairs)


def shift(value, axis, by):
    n = SIZES[AXES.index(axis)]
    return lax.ppermute(value, axis, [(i, (i + by) % n) for i in range(n)])


def halves(value):
    high = value.astype(jnp.bfloat16)
    low = (value - high.astype(jnp.float32)).astype(jnp.bfloat16)
    return high, low


def phase_and_size(table):
    size = jnp.max(jnp.max(jnp.abs(table), axis=0, keepdims=True), axis=1, keepdims=True)
    return jnp.where(table > 0, 1.0, jnp.where(table < 0, -1.0, 0.0)), size


def prepare_beta_kernel(*refs):
    tables, (phases, sizes) = refs[:-2], refs[-2:]
    for side in range(2):
        for rank in range(2 * FEW):
            phase, size = phase_and_size(tables[2 * side + rank // FEW][rank % FEW])
            phase = phase.T.astype(jnp.bfloat16)
            phases[side, rank, :B, :] = phase
            phases[side, rank, B:, :] = phase
            sizes[side, rank:rank + 1, :] = jnp.broadcast_to(size, (1, B))


def prepare_beta(*tables):
    count = 2 * FEW
    return pl.pallas_call(
        prepare_beta_kernel,
        out_shape=[jax.ShapeDtypeStruct((2, count, 2 * B, B), jnp.bfloat16), jax.ShapeDtypeStruct((2, count, B), jnp.float32)],
        compiler_params=pltpu.CompilerParams(vmem_limit_bytes=16 << 20),
        cost_estimate=pl.CostEstimate(flops=32 * B * B * 4, bytes_accessed=32 * B * B * 8, transcendentals=0),
        name="prepare_beta",
    )(*tables)


FEW = 8


def pack_kernel(place, links, counts, pairs, integrals, signs, out):
    first, is_source, yh = place[0] * 4, place[1] == 1, place[2]

    @pl.when(jnp.logical_not(is_source))
    def _():
        out[...] = jnp.zeros_like(out)

    @pl.when(is_source)
    def _():
        rank = jnp.int32(0)
        for i in range(4):
            for l in range(8):
                used = (l < counts[first + i]) & (((links[first + i, l] >> 2) & 1) == yh)

                @pl.when(used)
                def _(i=i, l=l, rank=rank):
                    pair = pairs[i, l]
                    out[jnp.minimum(rank, 2 * FEW - 1)] = signs[i, l].astype(jnp.float32) * integrals[pair >> 4, pair & 15]

                rank = rank + used.astype(jnp.int32)

        def clear(i, carry):
            out[i] = jnp.zeros((B, B), jnp.float32)
            return carry

        lax.fori_loop(rank, 2 * FEW, clear, 0)


def pack(place, links, counts, pairs, integrals, signs):
    scalar = pl.BlockSpec(memory_space=pltpu.SMEM)
    return pl.pallas_call(
        pack_kernel,
        out_shape=jax.ShapeDtypeStruct((2 * FEW, B, B), jnp.float32),
        in_specs=[scalar] * 5 + [pl.BlockSpec(memory_space=pltpu.VMEM)],
        out_specs=pl.BlockSpec(memory_space=pltpu.VMEM),
        compiler_params=pltpu.CompilerParams(vmem_limit_bytes=16 << 20),
        cost_estimate=pl.CostEstimate(flops=32 * B * B, bytes_accessed=48 * B * B * 4, transcendentals=0),
        name="pack",
    )(place, links, counts, pairs, integrals, signs)


def beta_kernel(place, links, counts, phases, sizes, *rest, spots):
    count = len(spots)
    pieces, (out, held, names, left, sems) = rest[:count], rest[count:]
    rows = out.shape[0]
    copies = [
        pltpu.make_async_copy(piece.at[pl.ds(start, size), :], held.at[slot, pl.ds(to, size), :], sems.at[i])
        for i, (piece, (slot, start, to, size)) in enumerate(zip(pieces, spots))
    ]
    for copy in copies:
        copy.start()
    z, yh, which = place[0], place[1], place[2]
    first = (z * 2 + which) * 4
    rank = jnp.int32(0)
    for r in range(2 * FEW):
        names[r] = 0
    for i in range(4):
        for l in range(8):
            source = links[first + i, l]
            used = (l < counts[first + i]) & (((source >> 2) & 1) == yh)

            @pl.when(used)
            def _(i=i, source=source, rank=rank):
                names[jnp.minimum(rank, 2 * FEW - 1)] = source * 4 + i

            rank = rank + used.astype(jnp.int32)
    out[...] = jnp.zeros_like(out)
    for copy in copies:
        copy.wait()
    for r in range(2 * FEW):
        name = names[r]
        slot = ((name >> 5) - z) & 7
        lanes = pl.ds(pl.multiple_of(((name >> 2) & 3) * B, B), B)
        target = pl.ds(pl.multiple_of((name & 3) * B, B), B)
        left[r % 2, :, :B], left[r % 2, :, B:] = halves(held[slot, :, lanes] * sizes[0, r:r + 1, :])
        out[:, target] += jnp.dot(left[r % 2], phases[0, r], preferred_element_type=jnp.float32)


def beta_part(place, links, counts, phases, sizes, rows, pieces, spots):
    return pl.pallas_call(
        functools.partial(beta_kernel, spots=spots),
        out_shape=jax.ShapeDtypeStruct((rows, 4 * B), jnp.float32),
        grid_spec=pltpu.PrefetchScalarGridSpec(
            num_scalar_prefetch=3,
            grid=(1,),
            in_specs=[
                pl.BlockSpec((1, 2 * FEW, 2 * B, B), lambda i, place, *_: (place[3], 0, 0, 0), pipeline_mode=pl.Buffered(1)),
                pl.BlockSpec((1, 2 * FEW, B), lambda i, place, *_: (place[3], 0, 0), pipeline_mode=pl.Buffered(1)),
            ] + [pl.BlockSpec(memory_space=pl.ANY)] * len(spots),
            out_specs=pl.BlockSpec((rows, 4 * B), lambda i, *_: (0, 0), pipeline_mode=pl.Buffered(1)),
            scratch_shapes=[
                pltpu.VMEM((8, rows, 4 * B), jnp.float32),
                pltpu.SMEM((2 * FEW,), jnp.int32),
                pltpu.VMEM((2, rows, 2 * B), jnp.bfloat16),
                pltpu.SemaphoreType.DMA((len(spots),)),
            ],
        ),
        compiler_params=pltpu.CompilerParams(dimension_semantics=("arbitrary",), vmem_limit_bytes=24 << 20),
        cost_estimate=pl.CostEstimate(flops=16 * rows * B * 2 * B * 2, bytes_accessed=rows * 512 * 36 + (1 << 20), transcendentals=0),
        name="beta",
    )(place, links, counts, phases, sizes, *pieces)


def alpha_kernel(place, links, counts, pairs, integrals, signs, *rest):
    tiles, (out, left, high, low) = rest[:8], rest[8:]
    step = pl.program_id(0)
    block = place[0] * 4 + step
    for l in range(8):
        pair = pairs[step, l]
        coef = jnp.where(l < counts[block], integrals[pair >> 4, pair & 15], 0.0)
        left[:, l * B:(l + 1) * B] = signs[0, l].astype(jnp.float32).astype(jnp.bfloat16)
        high[l * B:(l + 1) * B, :], low[l * B:(l + 1) * B, :] = halves(tiles[l][0] * coef)
    out[...] = jnp.dot(left[...], high[...], preferred_element_type=jnp.float32) + jnp.dot(
        left[...], low[...], preferred_element_type=jnp.float32
    )


def alpha_part(place, links, counts, pairs, integrals, signs, column):
    def tile(l):
        return pl.BlockSpec((1, B, 4 * B), lambda i, place, links, *_: (links[place[0] * 4 + i, l], 0, 0))

    return pl.pallas_call(
        alpha_kernel,
        out_shape=jax.ShapeDtypeStruct((4 * B, 4 * B), jnp.float32),
        grid_spec=pltpu.PrefetchScalarGridSpec(
            num_scalar_prefetch=5,
            grid=(4,),
            in_specs=[pl.BlockSpec((1, 8, B, B), lambda i, *_: (i, 0, 0, 0))] + [tile(l) for l in range(8)],
            out_specs=pl.BlockSpec((B, 4 * B), lambda i, *_: (i, 0)),
            scratch_shapes=[
                pltpu.VMEM((B, 8 * B), jnp.bfloat16),
                pltpu.VMEM((8 * B, 4 * B), jnp.bfloat16),
                pltpu.VMEM((8 * B, 4 * B), jnp.bfloat16),
            ],
        ),
        compiler_params=pltpu.CompilerParams(dimension_semantics=("arbitrary",), vmem_limit_bytes=VMEM_LIMIT),
        cost_estimate=pl.CostEstimate(flops=4 * 4 * B * B * 16 * B * 2, bytes_accessed=11 << 20, transcendentals=0),
        name="alpha",
    )(place, links, counts, pairs, integrals, signs, *[column] * 8)


HALF = 2 * B


def local(vector, one_electron, links, counts, pairs, signs):
    yl, x, c, z, yh = (lax.axis_index(a) for a in AXES)
    row_index = (yl * 4 + x) * 2 + c
    column = lax.all_gather(vector, ROW, axis=0, tiled=True).reshape(64, B, 4 * B)

    up, down = [vector], [vector]
    for _ in range(2):
        up.append(shift(up[-1], "z", 1))
        down.append(shift(down[-1], "z", -1))
    near = [vector, down[1], down[2], up[2], up[1]]
    chunks = []
    for n in range(2):
        rows = slice(n * HALF, (n + 1) * HALF)
        up3, down3 = shift(up[2][rows], "z", 1), shift(down[2][rows], "z", -1)
        far = [down3, shift(up3[:HALF // 2], "z", 1), shift(down3[HALF // 2:], "z", -1), up3]
        chunks.append(far)

    def near_spots(start, rows):
        return [(slot, start, 0, rows) for slot in (0, 1, 2, 6, 7)]

    def far_spots(to):
        return [(3, 0, to, HALF), (4, 0, to, HALF // 2), (4, 0, to + HALF // 2, HALF // 2), (5, 0, to, HALF)]

    is_source = (yl == z >> 2) & (x == z & 3)
    packed = pack(jnp.stack([row_index, is_source.astype(jnp.int32), yh]), links, counts, pairs, one_electron, signs)
    first, second = packed[:FEW], packed[FEW:]
    o, p, q, r = (0, 0), (0, 1), (0, 2), (0, 3)
    yo, yp, yq, yr = (1, 0), (1, 1), (1, 2), (1, 3)
    first += spread(first, [(o, yo)])
    first += spread(first, [(o, p), (yo, yp)])
    first += spread(first, [(o, r), (yo, yr), (p, q), (yp, yq)])
    second += spread(second, [(o, p)])
    second += spread(second, [(o, r), (p, q)])
    second += spread(second, [(o, yo), (p, yp), (q, yq), (r, yr)])
    phases, sizes = prepare_beta(first, second, shift(first, "c", 1), shift(second, "c", 1))

    theirs, ours = (jnp.stack([z, yh, which, (which ^ c)]).astype(jnp.int32) for which in (1 - yh, yh))
    tables = (links, counts, phases, sizes)
    partial = [
        beta_part(theirs, *tables, HALF, near + chunks[n], near_spots(n * HALF, HALF) + far_spots(0)) for n in range(2)
    ]
    sent = [shift(value, "yh", 1) for value in partial]
    ours, _ = lax.optimization_barrier((ours, partial[1]))
    kept = beta_part(ours, *tables, 2 * HALF, near + chunks[0] + chunks[1], near_spots(0, 2 * HALF) + far_spots(0) + far_spots(HALF))
    place, _ = lax.optimization_barrier((row_index[None].astype(jnp.int32), partial[1]))
    alpha = alpha_part(place, links, counts, pairs, one_electron, signs, column)
    return alpha + kept + jnp.concatenate(sent, axis=0)


def solution(mesh):
    fine = Mesh(mesh.devices.reshape(SIZES), AXES)
    in_specs = (P(ROW, COL), P(), P(), P(), P(ROW, None), P(ROW, None, None, None))
    return jax.shard_map(local, mesh=fine, in_specs=in_specs, out_specs=P(ROW, COL), check_vma=False)
```

```python
import functools

import jax
import jax.numpy as jnp
from jax import lax
from jax.experimental import pallas as pl
from jax.experimental.pallas import tpu as pltpu
from jax.sharding import Mesh, PartitionSpec as P

AXES = ("yl", "x", "c", "z", "yh")
SIZES = (2, 4, 2, 8, 2)
ROW = ("yl", "x", "c")
COL = ("z", "yh")
B = 128
VMEM_LIMIT = 60 * 1024 * 1024


def flat(yl, x, c, z, yh):
    return (((yl * 4 + x) * 2 + c) * 8 + z) * 2 + yh


def spread(value, moves):
    pairs = []
    for z in range(8):
        ys, xs = z >> 2, z & 3
        for yh in range(2):
            for c in range(2):
                for (ay, ax), (by, bx) in moves:
                    pairs.append((flat(ys ^ ay, (xs + ax) % 4, c, z, yh), flat(ys ^ by, (xs + bx) % 4, c, z, yh)))
    return lax.ppermute(value, AXES, pairs)


def shift(value, axis, by):
    n = SIZES[AXES.index(axis)]
    return lax.ppermute(value, axis, [(i, (i + by) % n) for i in range(n)])


def halves(value):
    high = value.astype(jnp.bfloat16)
    low = (value - high.astype(jnp.float32)).astype(jnp.bfloat16)
    return high, low


def phase_and_size(table):
    size = jnp.max(jnp.max(jnp.abs(table), axis=0, keepdims=True), axis=1, keepdims=True)
    return jnp.where(table > 0, 1.0, jnp.where(table < 0, -1.0, 0.0)), size


def prepare_beta_kernel(*refs):
    tables, (phases, sizes) = refs[:-2], refs[-2:]
    for side in range(2):
        for rank in range(2 * FEW):
            phase, size = phase_and_size(tables[2 * side + rank // FEW][rank % FEW])
            phase = phase.T.astype(jnp.bfloat16)
            phases[side, rank, :B, :] = phase
            phases[side, rank, B:, :] = phase
            sizes[side, rank:rank + 1, :] = jnp.broadcast_to(size, (1, B))


def prepare_beta(*tables):
    count = 2 * FEW
    return pl.pallas_call(
        prepare_beta_kernel,
        out_shape=[jax.ShapeDtypeStruct((2, count, 2 * B, B), jnp.bfloat16), jax.ShapeDtypeStruct((2, count, B), jnp.float32)],
        compiler_params=pltpu.CompilerParams(vmem_limit_bytes=16 << 20),
        cost_estimate=pl.CostEstimate(flops=32 * B * B * 4, bytes_accessed=32 * B * B * 8, transcendentals=0),
        name="prepare_beta",
    )(*tables)


FEW = 8


def pack_kernel(place, links, counts, pairs, integrals, signs, out):
    first, is_source, yh = place[0] * 4, place[1] == 1, place[2]

    @pl.when(jnp.logical_not(is_source))
    def _():
        out[...] = jnp.zeros_like(out)

    @pl.when(is_source)
    def _():
        rank = jnp.int32(0)
        for i in range(4):
            for l in range(8):
                used = (l < counts[first + i]) & (((links[first + i, l] >> 2) & 1) == yh)

                @pl.when(used)
                def _(i=i, l=l, rank=rank):
                    pair = pairs[i, l]
                    out[jnp.minimum(rank, 2 * FEW - 1)] = signs[i, l].astype(jnp.float32) * integrals[pair >> 4, pair & 15]

                rank = rank + used.astype(jnp.int32)

        def clear(i, carry):
            out[i] = jnp.zeros((B, B), jnp.float32)
            return carry

        lax.fori_loop(rank, 2 * FEW, clear, 0)


def pack(place, links, counts, pairs, integrals, signs):
    scalar = pl.BlockSpec(memory_space=pltpu.SMEM)
    return pl.pallas_call(
        pack_kernel,
        out_shape=jax.ShapeDtypeStruct((2 * FEW, B, B), jnp.float32),
        in_specs=[scalar] * 5 + [pl.BlockSpec(memory_space=pltpu.VMEM)],
        out_specs=pl.BlockSpec(memory_space=pltpu.VMEM),
        compiler_params=pltpu.CompilerParams(vmem_limit_bytes=16 << 20),
        cost_estimate=pl.CostEstimate(flops=32 * B * B, bytes_accessed=48 * B * B * 4, transcendentals=0),
        name="pack",
    )(place, links, counts, pairs, integrals, signs)


def beta_kernel(place, links, counts, phases, sizes, *rest, spots):
    count = len(spots)
    pieces, (out, held, names, sems) = rest[:count], rest[count:]
    rows = out.shape[0]
    copies = [
        pltpu.make_async_copy(piece.at[pl.ds(start, size), :], held.at[slot, pl.ds(to, size), :], sems.at[i])
        for i, (piece, (slot, start, to, size)) in enumerate(zip(pieces, spots))
    ]
    for copy in copies:
        copy.start()
    z, yh, which = place[0], place[1], place[2]
    first = (z * 2 + which) * 4
    rank = jnp.int32(0)
    for i in range(4):
        for l in range(8):
            source = links[first + i, l]
            names[jnp.minimum(rank, 2 * FEW)] = source * 4 + i
            rank = rank + ((l < counts[first + i]) & (((source >> 2) & 1) == yh)).astype(jnp.int32)

    for r in range(1, 2 * FEW):
        names[r] = jnp.where(r < rank, names[r], 0)
    out[...] = jnp.zeros_like(out)

    @pl.when(is_source)
    def _():
        rank = jnp.int32(0)
        for i in range(4):
            for l in range(8):
                used = (l < counts[first + i]) & (((links[first + i, l] >> 2) & 1) == yh)

                @pl.when(used)
                def _(i=i, l=l, rank=rank):
                    pair = pairs[i, l]
                    out[jnp.minimum(rank, 2 * FEW - 1)] = signs[i, l].astype(jnp.float32) * integrals[pair >> 4, pair & 15]

                rank = rank + used.astype(jnp.int32)

        def clear(i, carry):
            out[i] = jnp.zeros((B, B), jnp.float32)
            return carry

        lax.fori_loop(rank, 2 * FEW, clear, 0)


def pack(place, links, counts, pairs, integrals, signs):
    scalar = pl.BlockSpec(memory_space=pltpu.SMEM)
    return pl.pallas_call(
        pack_kernel,
        out_shape=jax.ShapeDtypeStruct((2 * FEW, B, B), jnp.float32),
        in_specs=[scalar] * 5 + [pl.BlockSpec(memory_space=pltpu.VMEM)],
        out_specs=pl.BlockSpec(memory_space=pltpu.VMEM),
        compiler_params=pltpu.CompilerParams(vmem_limit_bytes=16 << 20),
        cost_estimate=pl.CostEstimate(flops=32 * B * B, bytes_accessed=48 * B * B * 4, transcendentals=0),
        name="pack",
    )(place, links, counts, pairs, integrals, signs)


def beta_kernel(place, links, counts, phases, sizes, *rest, spots):
    count = len(spots)
    pieces, (out, held, names, sems) = rest[:count], rest[count:]
    rows = out.shape[0]
    copies = [
        pltpu.make_async_copy(piece.at[pl.ds(start, size), :], held.at[slot, pl.ds(to, size), :], sems.at[i])
        for i, (piece, (slot, start, to, size)) in enumerate(zip(pieces, spots))
    ]
    for copy in copies:
        copy.start()
    z, yh, which = place[0], place[1], place[2]
    first = (z * 2 + which) * 4
    rank = jnp.int32(0)
    for r in range(2 * FEW):
        names[r] = 0
    for i in range(4):
        for l in range(8):
            source = links[first + i, l]
            used = (l < counts[first + i]) & (((source >> 2) & 1) == yh)

            @pl.when(used)
            def _(i=i, source=source, rank=rank):
                names[jnp.minimum(rank, 2 * FEW - 1)] = source * 4 + i

            rank = rank + used.astype(jnp.int32)
    out[...] = jnp.zeros_like(out)
    for copy in copies:
        copy.wait()
    for r in range(2 * FEW):
        name = names[r]
        slot = ((name >> 5) - z) & 7
        lanes = pl.ds(pl.multiple_of(((name >> 2) & 3) * B, B), B)
        target = pl.ds(pl.multiple_of((name & 3) * B, B), B)
        for start in range(0, rows, B):
            tile = slice(start, start + B)
            both = jnp.concatenate(halves(held[slot, tile, lanes] * sizes[0, r:r + 1, :]), axis=1)
            out[tile, target] += jnp.dot(both, phases[0, r], preferred_element_type=jnp.float32)


def beta_part(place, links, counts, phases, sizes, rows, pieces, spots):
    return pl.pallas_call(
        functools.partial(beta_kernel, spots=spots),
        out_shape=jax.ShapeDtypeStruct((rows, 4 * B), jnp.float32),
        grid_spec=pltpu.PrefetchScalarGridSpec(
            num_scalar_prefetch=3,
            grid=(1,),
            in_specs=[
                pl.BlockSpec((1, 2 * FEW, 2 * B, B), lambda i, place, *_: (place[3], 0, 0, 0), pipeline_mode=pl.Buffered(1)),
                pl.BlockSpec((1, 2 * FEW, B), lambda i, place, *_: (place[3], 0, 0), pipeline_mode=pl.Buffered(1)),
            ] + [pl.BlockSpec(memory_space=pl.ANY)] * len(spots),
            out_specs=pl.BlockSpec((rows, 4 * B), lambda i, *_: (0, 0), pipeline_mode=pl.Buffered(1)),
            scratch_shapes=[
                pltpu.VMEM((8, rows, 4 * B), jnp.float32),
                pltpu.SMEM((2 * FEW + 1,), jnp.int32),
                pltpu.SemaphoreType.DMA((len(spots),)),
            ],
        ),
        compiler_params=pltpu.CompilerParams(dimension_semantics=("arbitrary",), vmem_limit_bytes=VMEM_LIMIT),
        cost_estimate=pl.CostEstimate(flops=16 * rows * B * 2 * B * 2, bytes_accessed=rows * 512 * 36 + (1 << 20), transcendentals=0),
        name="beta",
    )(place, links, counts, phases, sizes, *pieces)


def alpha_kernel(place, links, counts, pairs, integrals, signs, *rest):
    tiles, (kept, out) = rest[:8], rest[8:]
    step = pl.program_id(0)
    block = place[0] * 4 + step
    coefs = []
    for l in range(8):
        pair = pairs[step, l]
        coefs.append(jnp.where(l < counts[block], integrals[pair >> 4, pair & 15], 0.0))
    phase = jnp.concatenate([signs[0, k].astype(jnp.float32).astype(jnp.bfloat16) for k in range(8)], axis=1)
    for half in range(2):
        lanes = slice(half * 2 * B, (half + 1) * 2 * B)
        parts = [halves(tiles[k][0, :, lanes] * coefs[k]) for k in range(8)]
        right = jnp.concatenate([pair[0] for pair in parts], axis=0)
        total = kept[:, lanes] + jnp.dot(phase, right, preferred_element_type=jnp.float32)
        right = jnp.concatenate([pair[1] for pair in parts], axis=0)
        out[:, lanes] = total + jnp.dot(phase, right, preferred_element_type=jnp.float32)


def alpha_part(place, links, counts, pairs, integrals, signs, column, kept):
    def tile(l):
        return pl.BlockSpec((1, B, 4 * B), lambda i, place, links, *_: (links[place[0] * 4 + i, l], 0, 0))

    return pl.pallas_call(
        alpha_kernel,
        out_shape=jax.ShapeDtypeStruct((4 * B, 4 * B), jnp.float32),
        grid_spec=pltpu.PrefetchScalarGridSpec(
            num_scalar_prefetch=5,
            grid=(4,),
            in_specs=[pl.BlockSpec((1, 8, B, B), lambda i, *_: (i, 0, 0, 0))] + [tile(l) for l in range(8)] + [
                pl.BlockSpec((B, 4 * B), lambda i, *_: (i, 0)),
            ],
            out_specs=pl.BlockSpec((B, 4 * B), lambda i, *_: (i, 0)),
        ),
        compiler_params=pltpu.CompilerParams(dimension_semantics=("arbitrary",), vmem_limit_bytes=VMEM_LIMIT),
        cost_estimate=pl.CostEstimate(flops=4 * 4 * B * B * 16 * B * 2, bytes_accessed=14 << 20, transcendentals=0),
        name="alpha",
    )(place, links, counts, pairs, integrals, signs, *[column] * 8, kept)


HALF = 2 * B


def local(vector, one_electron, links, counts, pairs, signs):
    yl, x, c, z, yh = (lax.axis_index(a) for a in AXES)
    row_index = (yl * 4 + x) * 2 + c
    column = lax.all_gather(vector, ROW, axis=0, tiled=True).reshape(64, B, 4 * B)

    up, down = [vector], [vector]
    for _ in range(2):
        up.append(shift(up[-1], "z", 1))
        down.append(shift(down[-1], "z", -1))
    near = [vector, down[1], down[2], up[2], up[1]]
    chunks = []
    for n in range(2):
        rows = slice(n * HALF, (n + 1) * HALF)
        up3, down3 = shift(up[2][rows], "z", 1), shift(down[2][rows], "z", -1)
        far = [down3, shift(up3[:HALF // 2], "z", 1), shift(down3[HALF // 2:], "z", -1), up3]
        chunks.append(far)

    def near_spots(start, rows):
        return [(slot, start, 0, rows) for slot in (0, 1, 2, 6, 7)]

    def far_spots(to):
        return [(3, 0, to, HALF), (4, 0, to, HALF // 2), (4, 0, to + HALF // 2, HALF // 2), (5, 0, to, HALF)]

    is_source = (yl == z >> 2) & (x == z & 3)
    packed = pack(jnp.stack([row_index, is_source.astype(jnp.int32), yh]), links, counts, pairs, one_electron, signs)
    first, second = packed[:FEW], packed[FEW:]
    o, p, q, r = (0, 0), (0, 1), (0, 2), (0, 3)
    yo, yp, yq, yr = (1, 0), (1, 1), (1, 2), (1, 3)
    first += spread(first, [(o, yo)])
    first += spread(first, [(o, p), (yo, yp)])
    first += spread(first, [(o, r), (yo, yr), (p, q), (yp, yq)])
    second += spread(second, [(o, p)])
    second += spread(second, [(o, r), (p, q)])
    second += spread(second, [(o, yo), (p, yp), (q, yq), (r, yr)])
    phases, sizes = prepare_beta(first, second, shift(first, "c", 1), shift(second, "c", 1))

    theirs, ours = (jnp.stack([z, yh, which, (which ^ c)]).astype(jnp.int32) for which in (1 - yh, yh))
    tables = (links, counts, phases, sizes)
    partial = [
        beta_part(theirs, *tables, HALF, near + chunks[n], near_spots(n * HALF, HALF) + far_spots(0)) for n in range(2)
    ]
    sent = [shift(value, "yh", 1) for value in partial]
    ours, _ = lax.optimization_barrier((ours, partial[1]))
    kept = beta_part(ours, *tables, 2 * HALF, near + chunks[0] + chunks[1], near_spots(0, 2 * HALF) + far_spots(0) + far_spots(HALF))
    place = row_index[None].astype(jnp.int32)
    return alpha_part(place, links, counts, pairs, one_electron, signs, column, kept) + jnp.concatenate(sent, axis=0)


def solution(mesh):
    fine = Mesh(mesh.devices.reshape(SIZES), AXES)
    in_specs = (P(ROW, COL), P(), P(), P(), P(ROW, None), P(ROW, None, None, None))
    return jax.shard_map(local, mesh=fine, in_specs=in_specs, out_specs=P(ROW, COL), check_vma=False)
```

```python
import functools

import jax
import jax.numpy as jnp
from jax import lax
from jax.experimental import pallas as pl
from jax.experimental.pallas import tpu as pltpu
from jax.sharding import Mesh, PartitionSpec as P

AXES = ("yl", "x", "c", "z", "yh")
SIZES = (2, 4, 2, 8, 2)
ROW = ("yl", "x", "c")
COL = ("z", "yh")
B = 128
VMEM_LIMIT = 60 * 1024 * 1024


def flat(yl, x, c, z, yh):
    return (((yl * 4 + x) * 2 + c) * 8 + z) * 2 + yh


def spread(value, moves):
    pairs = []
    for z in range(8):
        ys, xs = z >> 2, z & 3
        for yh in range(2):
            for c in range(2):
                for (ay, ax), (by, bx) in moves:
                    pairs.append((flat(ys ^ ay, (xs + ax) % 4, c, z, yh), flat(ys ^ by, (xs + bx) % 4, c, z, yh)))
    return lax.ppermute(value, AXES, pairs)


def shift(value, axis, by):
    n = SIZES[AXES.index(axis)]
    return lax.ppermute(value, axis, [(i, (i + by) % n) for i in range(n)])


def pair_values(pair_ids, used, integrals):
    flat_table = integrals.reshape(-1)
    onehot = pair_ids[:, :, None] == jnp.arange(flat_table.shape[0], dtype=jnp.int32)[None, None, :]
    values = jnp.sum(jnp.where(onehot, flat_table[None, None, :], 0.0), axis=2)
    in_use = jnp.arange(pair_ids.shape[1], dtype=jnp.int32)[None, :] < used[:, None]
    return jnp.where(in_use, values, 0.0)


def halves(value):
    high = value.astype(jnp.bfloat16)
    low = (value - high.astype(jnp.float32)).astype(jnp.bfloat16)
    return high, low


def phase_and_size(table):
    size = jnp.max(jnp.max(jnp.abs(table), axis=0, keepdims=True), axis=1, keepdims=True)
    return jnp.where(table > 0, 1.0, jnp.where(table < 0, -1.0, 0.0)), size


def prepare_beta_kernel(*refs):
    tables, (phases, sizes) = refs[:-2], refs[-2:]
    for side in range(2):
        for rank in range(2 * FEW):
            phase, size = phase_and_size(tables[2 * side + rank // FEW][rank % FEW])
            phase = phase.T.astype(jnp.bfloat16)
            phases[side, rank, :B, :] = phase
            phases[side, rank, B:, :] = phase
            sizes[side, rank:rank + 1, :] = jnp.broadcast_to(size, (1, B))


def prepare_beta(*tables):
    count = 2 * FEW
    return pl.pallas_call(
        prepare_beta_kernel,
        out_shape=[jax.ShapeDtypeStruct((2, count, 2 * B, B), jnp.bfloat16), jax.ShapeDtypeStruct((2, count, B), jnp.float32)],
        compiler_params=pltpu.CompilerParams(vmem_limit_bytes=16 << 20),
        cost_estimate=pl.CostEstimate(flops=32 * B * B * 4, bytes_accessed=32 * B * B * 8, transcendentals=0),
        name="prepare_beta",
    )(*tables)


FEW = 8


def pack_kernel(place, links, counts, pairs, integrals, signs, out):
    first, is_source, yh = place[0] * 4, place[1] == 1, place[2]

    @pl.when(jnp.logical_not(is_source))
    def _():
        out[...] = jnp.zeros_like(out)

    @pl.when(is_source)
    def _():
        rank = jnp.int32(0)
        for i in range(4):
            for l in range(8):
                used = (l < counts[first + i]) & (((links[first + i, l] >> 2) & 1) == yh)

                @pl.when(used)
                def _(i=i, l=l, rank=rank):
                    pair = pairs[i, l]
                    out[jnp.minimum(rank, 2 * FEW - 1)] = signs[i, l].astype(jnp.float32) * integrals[pair >> 4, pair & 15]

                rank = rank + used.astype(jnp.int32)

        def clear(i, carry):
            out[i] = jnp.zeros((B, B), jnp.float32)
            return carry

        lax.fori_loop(rank, 2 * FEW, clear, 0)


def pack(place, links, counts, pairs, integrals, signs):
    scalar = pl.BlockSpec(memory_space=pltpu.SMEM)
    return pl.pallas_call(
        pack_kernel,
        out_shape=jax.ShapeDtypeStruct((2 * FEW, B, B), jnp.float32),
        in_specs=[scalar] * 5 + [pl.BlockSpec(memory_space=pltpu.VMEM)],
        out_specs=pl.BlockSpec(memory_space=pltpu.VMEM),
        compiler_params=pltpu.CompilerParams(vmem_limit_bytes=16 << 20),
        cost_estimate=pl.CostEstimate(flops=32 * B * B, bytes_accessed=48 * B * B * 4, transcendentals=0),
        name="pack",
    )(place, links, counts, pairs, integrals, signs)


def beta_kernel(names, phases, sizes, *rest, spots):
    count = len(spots)
    pieces, (out, held, sems) = rest[:count], rest[count:]
    rows = out.shape[0]
    copies = [
        pltpu.make_async_copy(piece.at[pl.ds(start, size), :], held.at[slot, pl.ds(to, size), :], sems.at[i])
        for i, (piece, (slot, start, to, size)) in enumerate(zip(pieces, spots))
    ]
    for copy in copies:
        copy.start()
    out[...] = jnp.zeros_like(out)
    for copy in copies:
        copy.wait()
    for r in range(2 * FEW):
        name = names[r]
        lanes = pl.ds(pl.multiple_of(((name >> 2) & 3) * B, B), B)
        target = pl.ds(pl.multiple_of((name & 3) * B, B), B)
        for start in range(0, rows, B):
            tile = slice(start, start + B)
            both = jnp.concatenate(halves(held[name >> 4, tile, lanes] * sizes[0, r:r + 1, :]), axis=1)
            out[tile, target] += jnp.dot(both, phases[0, r], preferred_element_type=jnp.float32)


def beta_names(links, counts, z, yh, which, c):
    first = (z * 2 + which) * 4
    source = lax.dynamic_slice_in_dim(links, first, 4).reshape(32)
    block = jnp.arange(32, dtype=jnp.int32) // 8
    link = jnp.arange(32, dtype=jnp.int32) % 8
    limit = jnp.broadcast_to(lax.dynamic_slice_in_dim(counts, first, 4)[:, None], (4, 8)).reshape(32)
    used = (link < limit) & (((source >> 2) & 1) == yh)
    before = jnp.arange(32)[None, :] < jnp.arange(32)[:, None]
    rank = jnp.sum(jnp.where(before & used[None, :], 1, 0), axis=1)
    name = (((source >> 3) - z) & 7) * 16 + (source & 3) * 4 + block
    at = used[None, :] & (rank[None, :] == jnp.arange(2 * FEW)[:, None])
    names = jnp.sum(jnp.where(at, name[None, :], 0), axis=1)
    return jnp.concatenate([names, (which ^ c)[None]]).astype(jnp.int32)


def beta_part(names, phases, sizes, rows, pieces, spots):
    return pl.pallas_call(
        functools.partial(beta_kernel, spots=spots),
        out_shape=jax.ShapeDtypeStruct((rows, 4 * B), jnp.float32),
        grid_spec=pltpu.PrefetchScalarGridSpec(
            num_scalar_prefetch=1,
            grid=(1,),
            in_specs=[
                pl.BlockSpec((1, 2 * FEW, 2 * B, B), lambda i, names: (names[2 * FEW], 0, 0, 0), pipeline_mode=pl.Buffered(1)),
                pl.BlockSpec((1, 2 * FEW, B), lambda i, names: (names[2 * FEW], 0, 0), pipeline_mode=pl.Buffered(1)),
            ] + [pl.BlockSpec(memory_space=pl.ANY)] * len(spots),
            out_specs=pl.BlockSpec((rows, 4 * B), lambda i, *_: (0, 0), pipeline_mode=pl.Buffered(1)),
            scratch_shapes=[
                pltpu.VMEM((8, rows, 4 * B), jnp.float32),
                pltpu.SemaphoreType.DMA((len(spots),)),
            ],
        ),
        compiler_params=pltpu.CompilerParams(dimension_semantics=("arbitrary",), vmem_limit_bytes=VMEM_LIMIT),
        cost_estimate=pl.CostEstimate(flops=16 * rows * B * 2 * B * 2, bytes_accessed=rows * 512 * 36 + (1 << 20), transcendentals=0),
        name="beta",
    )(names, phases, sizes, *pieces)


def alpha_kernel(blocks, coefs, signs, *rest):
    tiles, (kept, out) = rest[:8], rest[8:]
    coefs = [coefs[pl.program_id(0) * 8 + l] for l in range(8)]
    phase = jnp.concatenate([signs[0, k].astype(jnp.float32).astype(jnp.bfloat16) for k in range(8)], axis=1)
    for half in range(2):
        lanes = slice(half * 2 * B, (half + 1) * 2 * B)
        parts = [halves(tiles[k][0, :, lanes] * coefs[k]) for k in range(8)]
        right = jnp.concatenate([pair[0] for pair in parts], axis=0)
        total = kept[:, lanes] + jnp.dot(phase, right, preferred_element_type=jnp.float32)
        right = jnp.concatenate([pair[1] for pair in parts], axis=0)
        out[:, lanes] = total + jnp.dot(phase, right, preferred_element_type=jnp.float32)


def alpha_part(blocks, coefs, signs, column, kept):
    def tile(l):
        return pl.BlockSpec((1, B, 4 * B), lambda i, blocks, _: (blocks[i * 8 + l], 0, 0))

    return pl.pallas_call(
        alpha_kernel,
        out_shape=jax.ShapeDtypeStruct((4 * B, 4 * B), jnp.float32),
        grid_spec=pltpu.PrefetchScalarGridSpec(
            num_scalar_prefetch=2,
            grid=(4,),
            in_specs=[pl.BlockSpec((1, 8, B, B), lambda i, *_: (i, 0, 0, 0))] + [tile(l) for l in range(8)] + [
                pl.BlockSpec((B, 4 * B), lambda i, *_: (i, 0)),
            ],
            out_specs=pl.BlockSpec((B, 4 * B), lambda i, *_: (i, 0)),
        ),
        compiler_params=pltpu.CompilerParams(dimension_semantics=("arbitrary",), vmem_limit_bytes=VMEM_LIMIT),
        cost_estimate=pl.CostEstimate(flops=4 * 4 * B * B * 16 * B * 2, bytes_accessed=14 << 20, transcendentals=0),
        name="alpha",
    )(blocks, coefs, signs, *[column] * 8, kept)


HALF = 2 * B


def local(vector, one_electron, links, counts, pairs, signs):
    yl, x, c, z, yh = (lax.axis_index(a) for a in AXES)
    row_index = (yl * 4 + x) * 2 + c
    column = lax.all_gather(vector, ROW, axis=0, tiled=True).reshape(64, B, 4 * B)

    up, down = [vector], [vector]
    theirs, ours = (beta_names(links, counts, z, yh, which, c) for which in (1 - yh, yh))
    local_counts = lax.dynamic_slice_in_dim(counts, row_index * 4, 4)
    coefs = pair_values(pairs, local_counts, one_electron).reshape(32)
    blocks = lax.dynamic_slice_in_dim(links, row_index * 4, 4).reshape(32)
    up.append(shift(vector, "z", 1))
    down.append(shift(vector, "z", -1))
    (theirs, ours, coefs, blocks), up[1] = lax.optimization_barrier(((theirs, ours, coefs, blocks), up[1]))
    up.append(shift(up[-1], "z", 1))
    down.append(shift(down[-1], "z", -1))
    near = [vector, down[1], down[2], up[2], up[1]]
    chunks = []
    for n in range(2):
        rows = slice(n * HALF, (n + 1) * HALF)
        up3, down3 = shift(up[2][rows], "z", 1), shift(down[2][rows], "z", -1)
        far = [down3, shift(up3[:HALF // 2], "z", 1), shift(down3[HALF // 2:], "z", -1), up3]
        chunks.append(far)

    def near_spots(start, rows):
        return [(slot, start, 0, rows) for slot in (0, 1, 2, 6, 7)]

    def far_spots(to):
        return [(3, 0, to, HALF), (4, 0, to, HALF // 2), (4, 0, to + HALF // 2, HALF // 2), (5, 0, to, HALF)]

    is_source = (yl == z >> 2) & (x == z & 3)
    packed = pack(jnp.stack([row_index, is_source.astype(jnp.int32), yh]), links, counts, pairs, one_electron, signs)
    first, second = packed[:FEW], packed[FEW:]
    o, p, q, r = (0, 0), (0, 1), (0, 2), (0, 3)
    yo, yp, yq, yr = (1, 0), (1, 1), (1, 2), (1, 3)
    first += spread(first, [(o, yo)])
    first += spread(first, [(o, p), (yo, yp)])
    first += spread(first, [(o, r), (yo, yr), (p, q), (yp, yq)])
    second += spread(second, [(o, p)])
    second += spread(second, [(o, r), (p, q)])
    second += spread(second, [(o, yo), (p, yp), (q, yq), (r, yr)])
    phases, sizes = prepare_beta(first, second, shift(first, "c", 1), shift(second, "c", 1))

    tables = (phases, sizes)
    partial = [
        beta_part(theirs, *tables, HALF, near + chunks[n], near_spots(n * HALF, HALF) + far_spots(0)) for n in range(2)
    ]
    sent = [shift(value, "yh", 1) for value in partial]
    ours, _ = lax.optimization_barrier((ours, partial[1]))
    kept = beta_part(ours, *tables, 2 * HALF, near + chunks[0] + chunks[1], near_spots(0, 2 * HALF) + far_spots(0) + far_spots(HALF))
    return alpha_part(blocks, coefs, signs, column, kept) + jnp.concatenate(sent, axis=0)


def solution(mesh):
    fine = Mesh(mesh.devices.reshape(SIZES), AXES)
    in_specs = (P(ROW, COL), P(), P(), P(), P(ROW, None), P(ROW, None, None, None))
    return jax.shard_map(local, mesh=fine, in_specs=in_specs, out_specs=P(ROW, COL), check_vma=False)
```

```python
import functools

import jax
import jax.numpy as jnp
from jax import lax
from jax.experimental import pallas as pl
from jax.experimental.pallas import tpu as pltpu
from jax.sharding import Mesh, PartitionSpec as P

AXES = ("yl", "x", "c", "z", "yh")
SIZES = (2, 4, 2, 8, 2)
ROW = ("yl", "x", "c")
COL = ("z", "yh")
B = 128
VMEM_LIMIT = 60 * 1024 * 1024


def flat(yl, x, c, z, yh):
    return (((yl * 4 + x) * 2 + c) * 8 + z) * 2 + yh


def spread(value, moves):
    pairs = []
    for z in range(8):
        ys, xs = z >> 2, z & 3
        for yh in range(2):
            for c in range(2):
                for (ay, ax), (by, bx) in moves:
                    pairs.append((flat(ys ^ ay, (xs + ax) % 4, c, z, yh), flat(ys ^ by, (xs + bx) % 4, c, z, yh)))
    return lax.ppermute(value, AXES, pairs)


def shift(value, axis, by):
    n = SIZES[AXES.index(axis)]
    return lax.ppermute(value, axis, [(i, (i + by) % n) for i in range(n)])


def pair_values(pair_ids, used, integrals):
    flat_table = integrals.reshape(-1)
    onehot = pair_ids[:, :, None] == jnp.arange(flat_table.shape[0], dtype=jnp.int32)[None, None, :]
    values = jnp.sum(jnp.where(onehot, flat_table[None, None, :], 0.0), axis=2)
    in_use = jnp.arange(pair_ids.shape[1], dtype=jnp.int32)[None, :] < used[:, None]
    return jnp.where(in_use, values, 0.0)


def halves(value):
    high = value.astype(jnp.bfloat16)
    low = (value - high.astype(jnp.float32)).astype(jnp.bfloat16)
    return high, low


def phase_and_size(table):
    size = jnp.max(jnp.max(jnp.abs(table), axis=0, keepdims=True), axis=1, keepdims=True)
    return jnp.where(table > 0, 1.0, jnp.where(table < 0, -1.0, 0.0)), size


def prepare_beta_kernel(*refs):
    tables, (phases, sizes) = refs[:-2], refs[-2:]
    for side in range(2):
        for rank in range(2 * FEW):
            phase, size = phase_and_size(tables[2 * side + rank // FEW][rank % FEW])
            phase = phase.T.astype(jnp.bfloat16)
            phases[side, rank, :B, :] = phase
            phases[side, rank, B:, :] = phase
            sizes[side, rank:rank + 1, :] = jnp.broadcast_to(size, (1, B))


def prepare_beta(*tables):
    count = 2 * FEW
    return pl.pallas_call(
        prepare_beta_kernel,
        out_shape=[jax.ShapeDtypeStruct((2, count, 2 * B, B), jnp.bfloat16), jax.ShapeDtypeStruct((2, count, B), jnp.float32)],
        compiler_params=pltpu.CompilerParams(vmem_limit_bytes=16 << 20),
        cost_estimate=pl.CostEstimate(flops=32 * B * B * 4, bytes_accessed=32 * B * B * 8, transcendentals=0),
        name="prepare_beta",
    )(*tables)


FEW = 8


def pack_kernel(place, links, counts, pairs, integrals, signs, *outs):
    first, is_source, yh = place[0] * 4, place[1] == 1, place[2]

    @pl.when(jnp.logical_not(is_source))
    def _():
        for out in outs:
            out[...] = jnp.zeros_like(out)

    @pl.when(is_source)
    def _():
        rank = jnp.int32(0)
        for i in range(4):
            for l in range(8):
                used = (l < counts[first + i]) & (((links[first + i, l] >> 2) & 1) == yh)

                for half, out in enumerate(outs):

                    @pl.when(used & (rank // FEW == half))
                    def _(i=i, l=l, rank=rank, half=half, out=out):
                        pair = pairs[i, l]
                        out[rank - half * FEW] = signs[i, l].astype(jnp.float32) * integrals[pair >> 4, pair & 15]

                rank = rank + used.astype(jnp.int32)

        for half, out in enumerate(outs):

            def clear(i, carry, out=out):
                out[i] = jnp.zeros((B, B), jnp.float32)
                return carry

            lax.fori_loop(jnp.clip(rank - half * FEW, 0, FEW), FEW, clear, 0)


def pack(place, links, counts, pairs, integrals, signs):
    scalar = pl.BlockSpec(memory_space=pltpu.SMEM)
    return pl.pallas_call(
        pack_kernel,
        out_shape=[jax.ShapeDtypeStruct((FEW, B, B), jnp.float32)] * 2,
        in_specs=[scalar] * 5 + [pl.BlockSpec(memory_space=pltpu.VMEM)],
        out_specs=[pl.BlockSpec(memory_space=pltpu.VMEM)] * 2,
        compiler_params=pltpu.CompilerParams(vmem_limit_bytes=16 << 20),
        cost_estimate=pl.CostEstimate(flops=32 * B * B, bytes_accessed=48 * B * B * 4, transcendentals=0),
        name="pack",
    )(place, links, counts, pairs, integrals, signs)


def beta_kernel(names, phases, sizes, *rest, spots):
    count = len(spots)
    pieces, (out, held, sems) = rest[:count], rest[count:]
    rows = out.shape[0]
    copies = [
        pltpu.make_async_copy(piece.at[pl.ds(start, size), :], held.at[slot, pl.ds(to, size), :], sems.at[i])
        for i, (piece, (slot, start, to, size)) in enumerate(zip(pieces, spots))
    ]
    for copy in copies:
        copy.start()
    out[...] = jnp.zeros_like(out)
    for copy in copies:
        copy.wait()
    for r in range(2 * FEW):
        name = names[r]
        lanes = pl.ds(pl.multiple_of(((name >> 2) & 3) * B, B), B)
        target = pl.ds(pl.multiple_of((name & 3) * B, B), B)
        for start in range(0, rows, B):
            tile = slice(start, start + B)
            both = jnp.concatenate(halves(held[name >> 4, tile, lanes] * sizes[0, r:r + 1, :]), axis=1)
            out[tile, target] += jnp.dot(both, phases[0, r], preferred_element_type=jnp.float32)


def beta_names(links, counts, z, yh, which, c):
    first = (z * 2 + which) * 4
    source = lax.dynamic_slice_in_dim(links, first, 4).reshape(32)
    block = jnp.arange(32, dtype=jnp.int32) // 8
    link = jnp.arange(32, dtype=jnp.int32) % 8
    limit = jnp.broadcast_to(lax.dynamic_slice_in_dim(counts, first, 4)[:, None], (4, 8)).reshape(32)
    used = (link < limit) & (((source >> 2) & 1) == yh)
    before = jnp.arange(32)[None, :] < jnp.arange(32)[:, None]
    rank = jnp.sum(jnp.where(before & used[None, :], 1, 0), axis=1)
    name = (((source >> 3) - z) & 7) * 16 + (source & 3) * 4 + block
    at = used[None, :] & (rank[None, :] == jnp.arange(2 * FEW)[:, None])
    names = jnp.sum(jnp.where(at, name[None, :], 0), axis=1)
    return jnp.concatenate([names, (which ^ c)[None]]).astype(jnp.int32)


def beta_part(names, phases, sizes, rows, pieces, spots):
    return pl.pallas_call(
        functools.partial(beta_kernel, spots=spots),
        out_shape=jax.ShapeDtypeStruct((rows, 4 * B), jnp.float32),
        grid_spec=pltpu.PrefetchScalarGridSpec(
            num_scalar_prefetch=1,
            grid=(1,),
            in_specs=[
                pl.BlockSpec((1, 2 * FEW, 2 * B, B), lambda i, names: (names[2 * FEW], 0, 0, 0), pipeline_mode=pl.Buffered(1)),
                pl.BlockSpec((1, 2 * FEW, B), lambda i, names: (names[2 * FEW], 0, 0), pipeline_mode=pl.Buffered(1)),
            ] + [pl.BlockSpec(memory_space=pl.ANY)] * len(spots),
            out_specs=pl.BlockSpec((rows, 4 * B), lambda i, *_: (0, 0), pipeline_mode=pl.Buffered(1)),
            scratch_shapes=[
                pltpu.VMEM((8, rows, 4 * B), jnp.float32),
                pltpu.SemaphoreType.DMA((len(spots),)),
            ],
        ),
        compiler_params=pltpu.CompilerParams(dimension_semantics=("arbitrary",), vmem_limit_bytes=VMEM_LIMIT),
        cost_estimate=pl.CostEstimate(flops=16 * rows * B * 2 * B * 2, bytes_accessed=rows * 512 * 36 + (1 << 20), transcendentals=0),
        name="beta",
    )(names, phases, sizes, *pieces)


def alpha_kernel(blocks, coefs, signs, *rest):
    tiles, (kept, out) = rest[:8], rest[8:]
    coefs = [coefs[pl.program_id(0) * 8 + l] for l in range(8)]
    phase = jnp.concatenate([signs[0, k].astype(jnp.float32).astype(jnp.bfloat16) for k in range(8)], axis=1)
    for half in range(2):
        lanes = slice(half * 2 * B, (half + 1) * 2 * B)
        parts = [halves(tiles[k][0, :, lanes] * coefs[k]) for k in range(8)]
        right = jnp.concatenate([pair[0] for pair in parts], axis=0)
        total = kept[:, lanes] + jnp.dot(phase, right, preferred_element_type=jnp.float32)
        right = jnp.concatenate([pair[1] for pair in parts], axis=0)
        out[:, lanes] = total + jnp.dot(phase, right, preferred_element_type=jnp.float32)


def alpha_part(blocks, coefs, signs, column, kept):
    def tile(l):
        return pl.BlockSpec((1, B, 4 * B), lambda i, blocks, _: (blocks[i * 8 + l], 0, 0))

    return pl.pallas_call(
        alpha_kernel,
        out_shape=jax.ShapeDtypeStruct((4 * B, 4 * B), jnp.float32),
        grid_spec=pltpu.PrefetchScalarGridSpec(
            num_scalar_prefetch=2,
            grid=(4,),
            in_specs=[pl.BlockSpec((1, 8, B, B), lambda i, *_: (i, 0, 0, 0))] + [tile(l) for l in range(8)] + [
                pl.BlockSpec((B, 4 * B), lambda i, *_: (i, 0)),
            ],
            out_specs=pl.BlockSpec((B, 4 * B), lambda i, *_: (i, 0)),
        ),
        compiler_params=pltpu.CompilerParams(dimension_semantics=("arbitrary",), vmem_limit_bytes=VMEM_LIMIT),
        cost_estimate=pl.CostEstimate(flops=4 * 4 * B * B * 16 * B * 2, bytes_accessed=14 << 20, transcendentals=0),
        name="alpha",
    )(blocks, coefs, signs, *[column] * 8, kept)


HALF = 2 * B


def local(vector, one_electron, links, counts, pairs, signs):
    yl, x, c, z, yh = (lax.axis_index(a) for a in AXES)
    row_index = (yl * 4 + x) * 2 + c
    column = lax.all_gather(vector, ROW, axis=0, tiled=True).reshape(64, B, 4 * B)

    up, down = [vector], [vector]
    theirs, ours = (beta_names(links, counts, z, yh, which, c) for which in (1 - yh, yh))
    local_counts = lax.dynamic_slice_in_dim(counts, row_index * 4, 4)
    coefs = pair_values(pairs, local_counts, one_electron).reshape(32)
    blocks = lax.dynamic_slice_in_dim(links, row_index * 4, 4).reshape(32)
    up.append(shift(vector, "z", 1))
    down.append(shift(vector, "z", -1))
    (theirs, ours, coefs, blocks), up[1] = lax.optimization_barrier(((theirs, ours, coefs, blocks), up[1]))
    up.append(shift(up[-1], "z", 1))
    down.append(shift(down[-1], "z", -1))
    near = [vector, down[1], down[2], up[2], up[1]]
    chunks = []
    for n in range(2):
        rows = slice(n * HALF, (n + 1) * HALF)
        up3, down3 = shift(up[2][rows], "z", 1), shift(down[2][rows], "z", -1)
        far = [down3, shift(up3[:HALF // 2], "z", 1), shift(down3[HALF // 2:], "z", -1), up3]
        chunks.append(far)

    def near_spots(start, rows):
        return [(slot, start, 0, rows) for slot in (0, 1, 2, 6, 7)]

    def far_spots(to):
        return [(3, 0, to, HALF), (4, 0, to, HALF // 2), (4, 0, to + HALF // 2, HALF // 2), (5, 0, to, HALF)]

    is_source = (yl == z >> 2) & (x == z & 3)
    first, second = pack(jnp.stack([row_index, is_source.astype(jnp.int32), yh]), links, counts, pairs, one_electron, signs)
    o, p, q, r = (0, 0), (0, 1), (0, 2), (0, 3)
    yo, yp, yq, yr = (1, 0), (1, 1), (1, 2), (1, 3)
    first += spread(first, [(o, yo)])
    first += spread(first, [(o, p), (yo, yp)])
    first += spread(first, [(o, r), (yo, yr), (p, q), (yp, yq)])
    second += spread(second, [(o, p)])
    second += spread(second, [(o, r), (p, q)])
    second += spread(second, [(o, yo), (p, yp), (q, yq), (r, yr)])
    phases, sizes = prepare_beta(first, second, shift(first, "c", 1), shift(second, "c", 1))

    tables = (phases, sizes)
    partial = [
        beta_part(theirs, *tables, HALF, near + chunks[n], near_spots(n * HALF, HALF) + far_spots(0)) for n in range(2)
    ]
    sent = [shift(value, "yh", 1) for value in partial]
    ours, _ = lax.optimization_barrier((ours, partial[1]))
    kept = beta_part(ours, *tables, 2 * HALF, near + chunks[0] + chunks[1], near_spots(0, 2 * HALF) + far_spots(0) + far_spots(HALF))
    return alpha_part(blocks, coefs, signs, column, kept) + jnp.concatenate(sent, axis=0)


def solution(mesh):
    fine = Mesh(mesh.devices.reshape(SIZES), AXES)
    in_specs = (P(ROW, COL), P(), P(), P(), P(ROW, None), P(ROW, None, None, None))
    return jax.shard_map(local, mesh=fine, in_specs=in_specs, out_specs=P(ROW, COL), check_vma=False)
```
